128 devices in a mesh: batch: 2 (over x_hi), space: 64 (over z, y, x_lo, core).
Axes of the slice: x: 4 (x_hi: 2, x_lo: 2; x = x_hi * 2 + x_lo), y: 4, z: 4, core: 2. Of those that a mesh axis runs over, the one named last changes fastest.
Arguments:
- courant: float32 [512, 16, 256], P('space'), may hold values from 0.06 to 0.18
- wavelet: float32 [2, 256, 7], P('batch'), may hold values from -6 to 6
- source_owner: int32 [2, 256], P('batch'), may hold values from 0 to 63
- source_cell: int32 [2, 256], P('batch'), may hold values from 0 to 32767
- traces: float32 [2, 16384, 7], P('batch', 'space'), may hold values from -6 to 6
- station_owner: int32 [2, 16384, 1], P('batch', 'space'), may hold values from 0 to 63; in each aligned block of 256 rows (0 to 255, 256 to 511, ..., all dimensions but the last counted through in order) at most 8 rows name the same one
- station_cell: int32 [2, 16384], P('batch', 'space'), may hold values from 0 to 32767
Outputs:
- update: float32 [512, 16, 256], P('space', 'batch')
- agreement: float32 [1], replicated
The draws below stay inside these ranges and needn't reach their ends.
Inputs may be any that keep to these rules, and one draw needn't show every extreme that they name: `station_owner`: among the 256 trace rows of one device, at most 8 name the same owner, and in every draw some device reaches 8 for some owner.
All inputs are finite; a program needn't handle non-finite values.
Results may differ from the reference program's by a relative error of at most 0.0003.
Values sent between devices are 32-bit elements; how exact they have to be, the bound alone decides.
No kernel may reach another device: no remote copies, remote signals or barrier semaphores. Data moves between devices by JAX's collectives and lax.ppermute only.
A program may use at most 64 MiB of HBM per device.

```python
import math
import jax
import jax.numpy as jnp
import numpy as np

CX = 8
CY = 16
CZ = 256
STEPS = 7
STA_DEV = 256
BATCHES = 2
NX = 512
SRC = 256
STATIONS = 16384
CAP = 8
N_SPACE = 64


def set_ends(array, rng, least, largest):
    longest = array.shape.index(max(array.shape))
    spots = []
    for shift in (0, 1):
        where = [jax.random.randint(jax.random.fold_in(rng, axis), (), 0, length) for axis, length in enumerate(array.shape)]
        where[longest] = (where[longest] + shift) % array.shape[longest]
        spots.append(tuple(where))
    return array.at[spots[0]].set(least).at[spots[1]].set(largest)


def block_levels(key, shape, split, low, high):
    gain, own = 1.0, jax.random.fold_in(key, 6)
    for axis_at, parts in split:
        draws = jnp.exp(jax.random.uniform(jax.random.fold_in(own, axis_at), (parts,), jnp.float32, low / len(split), high / len(split)))
        gain = gain * jnp.repeat(draws, shape[axis_at] // parts).reshape([-1 if axis == axis_at else 1 for axis in range(len(shape))])
    return gain


def assign_block(stream_key, own, number, rows, number_of, top, bound, lean):
    order = jax.random.permutation(stream_key, number_of)
    packed, usual = portions_of(number_of, rows * top, bound, lean, True), portions_of(number_of, rows * top, bound, lean, False)
    places = jnp.arange(number_of)

    def named(sizes, offset_by):
        used = int((sizes > 0).sum())
        fixed = max(1, used // 4)
        shifted = fixed + (places - fixed + offset_by * (used - fixed)) % max(1, number_of - fixed)
        return jnp.zeros((number_of,), jnp.int32).at[order[jnp.where(places < fixed, places, shifted)]].set(jnp.asarray(sizes, jnp.int32))

    sizes = jnp.where(number % 4 == 0, named(packed, number // 4), named(usual, number - number // 4 - 1))
    mixed = jax.random.permutation(jax.random.fold_in(own, 3), number_of)
    giver, receiver = mixed[0:number_of // 2 * 2:2], mixed[1:number_of // 2 * 2:2]
    slack = jnp.minimum(sizes[giver] - 1, bound - sizes[receiver]) // 2
    slack = jnp.where((giver == order[0]) | (receiver == order[0]) | (sizes[receiver] == 0), 0, jnp.maximum(slack, 0))
    shifted = jax.random.randint(jax.random.fold_in(own, 4), (number_of // 2,), 0, 1 << 20) % (slack + 1)
    sizes = sizes.at[giver].add(-shifted).at[receiver].add(shifted)
    members = jnp.searchsorted(jnp.cumsum(sizes), jnp.arange(rows * top), side="right").astype(jnp.int32)
    grid = members.reshape(top, rows).T
    grid = grid[jax.random.permutation(jax.random.fold_in(own, 1), rows)]
    offset_by = jax.random.randint(jax.random.fold_in(own, 2), (rows, 1), 0, top)
    return jnp.take_along_axis(grid, (jnp.arange(top)[None, :] + offset_by) % top, axis=1)


def portions_of(amount, total, most, slope, full):
    weights = [(1 << 20) // math.isqrt(rank ** slope) + 1 for rank in range(1, amount + 1)]
    largest = most if full else min(most, max(-(-total // amount), total * weights[0] // sum(weights)))
    least = 1 if total - largest >= amount - 1 else 0
    holding, spare = [largest] + [least] * (amount - 1), total - largest - least * (amount - 1)
    while spare > 0:
        free = [i for i in range(1, amount) if holding[i] < largest] or [i for i in range(1, amount) if holding[i] < most]
        mass, remaining = sum([weights[i] for i in free]), spare
        for i in free:
            addition = min(most - holding[i], max(1, remaining * weights[i] // mass), spare)
            holding[i] = holding[i] + addition
            spare = spare - addition
    return np.array(holding)


def normal_values(key, extent, width, bound, pieces=(), kind=jnp.bfloat16):
    level = block_levels(key, extent, pieces, -0.22, 0.18) if pieces else 1.0
    values = jax.random.normal(key, extent, jnp.float32) * width * level
    return jnp.minimum(jnp.maximum(values, -bound), bound).astype(kind)


def setup_inputs(seed: int = 0) -> dict:
    splits = jax.random.split(jax.random.key(seed), 8)
    courant = jnp.clip(0.06 + 0.120000008 * jax.random.uniform(splits[0], (NX, CY, CZ), jnp.float32) ** block_levels(splits[0], (NX, CY, CZ), ((0, 64),), -0.2, 0.2), 0.06, 0.18)
    wavelet = normal_values(splits[1], (BATCHES, SRC, STEPS), 1.0, 6.0, ((0, 2),), jnp.float32)
    source_owner = set_ends(jax.random.randint(splits[2], (BATCHES, SRC), 0, N_SPACE), jax.random.fold_in(splits[2], 1), 0, N_SPACE - 1).astype(jnp.int32)
    source_cell = set_ends(jax.random.randint(splits[3], (BATCHES, SRC), 0, CX * CY * CZ), jax.random.fold_in(splits[3], 1), 0, (CX * CY * CZ) - 1).astype(jnp.int32)
    traces = normal_values(splits[4], (BATCHES, STATIONS, STEPS), 1.0, 6.0, ((0, 2), (1, 64)), jnp.float32)
    station_owner_keys = jax.random.split(jax.random.fold_in(splits[5], 1), BATCHES * STATIONS // STA_DEV)
    station_owner_turns = jax.random.permutation(jax.random.fold_in(splits[5], 3), BATCHES * STATIONS // STA_DEV)
    station_owner = jax.vmap(lambda own, number: assign_block(jax.random.fold_in(splits[5], 2), own, number, STA_DEV, N_SPACE, 1, CAP, 2))(station_owner_keys, station_owner_turns).reshape((BATCHES, STATIONS, 1))
    station_cell = set_ends(jax.random.randint(splits[6], (BATCHES, STATIONS), 0, CX * CY * CZ), jax.random.fold_in(splits[6], 1), 0, (CX * CY * CZ) - 1).astype(jnp.int32)
    return {"courant": courant, "wavelet": wavelet, "source_owner": source_owner, "source_cell": source_cell, "traces": traces, "station_owner": station_owner, "station_cell": station_cell}


center_tap = -205.0 / 72.0
stencil_taps = (1.6, -0.2, 8.0 / 315.0, -1.0 / 560.0)
epsilon = 1e-06

def laplace_rows(extended, height):
    span_y = extended.shape[1] - 8
    span_z = extended.shape[2] - 8

    def window(first, second, third):
        return extended[first:first + height, second:second + span_y, third:third + span_z]
    accumulated = 3.0 * center_tap * window(4, 4, 4)
    for offset in range(1, 5):
        neighbours = window(4 + offset, 4, 4) + window(4 - offset, 4, 4)
        neighbours = neighbours + window(4, 4 + offset, 4) + window(4, 4 - offset, 4)
        neighbours = neighbours + window(4, 4, 4 + offset) + window(4, 4, 4 - offset)
        accumulated = accumulated + stencil_taps[offset - 1] * neighbours
    return accumulated

def pad_all(wave_field):
    return jnp.pad(wave_field, ((4, 4), (4, 4), (4, 4)))

def inject(wave_field, positions, amounts):
    flattened = wave_field.reshape(-1)
    return flattened.at[positions].add(amounts).reshape(wave_field.shape)

def reference(courant, wavelet, source_owner, source_cell, traces, station_owner, station_cell):
    volume = CX * CY * CZ
    grid_shape = (NX, CY, CZ)
    gradients = []
    for member in range(BATCHES):
        source_flat = source_owner[member].astype(jnp.int32) * volume + source_cell[member].astype(jnp.int32)
        station_flat = station_owner[member, :, 0].astype(jnp.int32) * volume + station_cell[member].astype(jnp.int32)
        zero_field = jnp.zeros(grid_shape, jnp.float32)
        snapshots = [zero_field, inject(zero_field, source_flat, wavelet[member, :, 0])]
        for moment in range(1, STEPS):
            current = snapshots[moment]
            following = 2.0 * current - snapshots[moment - 1] + courant * laplace_rows(pad_all(current), NX)
            snapshots.append(inject(following, source_flat, wavelet[member, :, moment]))
        adjoint = inject(zero_field, station_flat, traces[member, :, STEPS - 1])
        previous_adjoint = zero_field
        gradient = adjoint * (snapshots[STEPS] - 2.0 * snapshots[STEPS - 1] + snapshots[STEPS - 2])
        for moment in range(STEPS - 2, 0, -1):
            newer = 2.0 * adjoint - previous_adjoint + laplace_rows(pad_all(courant * adjoint), NX)
            newer = inject(newer, station_flat, traces[member, :, moment])
            previous_adjoint, adjoint = (adjoint, newer)
            gradient = gradient + adjoint * (snapshots[moment + 1] - 2.0 * snapshots[moment] + snapshots[moment - 1])
        gradients.append(gradient)
    cells = float(NX * CY * CZ)
    mean_first = jnp.sum(gradients[0] * gradients[0]) / cells
    mean_second = jnp.sum(gradients[1] * gradients[1]) / cells
    update = (gradients[0] + gradients[1]) / jnp.sqrt((mean_first + mean_second) / 2.0 + epsilon)
    share = (mean_first + epsilon) / (mean_first + mean_second + 2.0 * epsilon)
    return (update, jnp.stack([share]))
```

```python
import jax
import jax.numpy as jnp
import numpy as np
from jax import lax
from jax.experimental import pallas as pl
from jax.experimental.pallas import tpu as pltpu
from jax.sharding import PartitionSpec as P

F32, BF16, I32 = jnp.float32, jnp.bfloat16, jnp.int32
center_tap = -205.0 / 72.0
stencil_taps = (1.6, -0.2, 8.0 / 315.0, -1.0 / 560.0)
epsilon = 1e-06

CX, CY, CZ = 8, 16, 256
BLK = CX * CY
REACH = 3
EXT = (2 * REACH + 1) * BLK
MID = REACH * BLK
STEPS = 7
SRC = 256
ROWS = 256
SLOTS = 8
PEERS = 64


def split2(x):
    hi = x.astype(BF16)
    return hi, (x - hi.astype(F32)).astype(BF16)


def taps():
    coeff = [0.0] + list(stencil_taps)
    band_xy = np.zeros((BLK, 2 * BLK), np.float64)
    for x in range(CX):
        for y in range(CY):
            row = x * CY + y
            band_xy[row, (x + 4) * CY + y] += 3.0 * center_tap
            for k in range(1, 5):
                band_xy[row, (x + 4 + k) * CY + y] += coeff[k]
                band_xy[row, (x + 4 - k) * CY + y] += coeff[k]
                for other in (y + k, y - k):
                    if 0 <= other < CY:
                        band_xy[row, (x + 4) * CY + other] += coeff[k]
    band_z = np.zeros((CZ, CZ), np.float64)
    for z in range(CZ):
        for k in range(1, 5):
            for other in (z + k, z - k):
                if 0 <= other < CZ:
                    band_z[other, z] += coeff[k]
    out = []
    for band in (band_xy, band_z):
        hi = band.astype(jnp.bfloat16)
        out += [hi, (band - hi.astype(np.float64)).astype(jnp.bfloat16)]
    return out


def dot(a, b):
    return lax.dot_general(a, b, (((1,), (0,)), ((), ())), preferred_element_type=F32)


def dot_nt(a, b):
    return lax.dot_general(a, b, (((1,), (1,)), ((), ())), preferred_element_type=F32)


def one_hot(index_row, height, base=0):
    iota = lax.broadcasted_iota(I32, (height, index_row.shape[1]), 0) + base
    return jnp.where(iota == index_row, 1.0, 0.0).astype(BF16)


def prep_kernel(traces, owner, cell, out, words, padded):
    own = owner[...]
    own_f = own.astype(F32)
    column = jnp.broadcast_to(own_f, (128, ROWS)).T
    column = jnp.concatenate([column, column], axis=1)
    first = lax.broadcasted_iota(I32, (ROWS, ROWS), 0)
    second = lax.broadcasted_iota(I32, (ROWS, ROWS), 1)
    same = (column == jnp.broadcast_to(own_f, (ROWS, ROWS))) & (first < second)
    rank = jnp.sum(jnp.where(same, 1.0, 0.0), axis=0, keepdims=True).astype(I32)
    half = SLOTS // 2
    low = rank < half
    place = own * half + jnp.where(low, rank, rank - half)
    hot_low = one_hot(jnp.where(low, place, -1), PEERS * half)
    hot_high = one_hot(jnp.where(low, -1, place), PEERS * half)
    hot = jnp.concatenate([hot_low, hot_high], axis=1)
    for t in range(1, STEPS):
        words[t - 1 : t, :] = traces[t]
    words[6:7, :] = cell[...].astype(F32)
    words[7:8, :] = jnp.zeros((1, ROWS), F32)
    rest = words[...]
    total = None
    for _ in range(3):
        piece = rest.astype(BF16)
        rest = rest - piece.astype(F32)
        wide = jnp.concatenate([piece.astype(F32)] * 8, axis=0)
        empty = jnp.zeros_like(wide)
        both = jnp.concatenate(
            [jnp.concatenate([wide, empty], axis=1), jnp.concatenate([empty, wide], axis=1)], axis=0
        ).astype(BF16)
        part = dot_nt(hot, both)
        total = part if total is None else total + part
    edge = 16
    padded[0:edge, :] = jnp.zeros((edge, 128), F32)
    padded[edge + ROWS : edge + ROWS + edge, :] = jnp.zeros((edge, 128), F32)
    padded[edge : edge + ROWS, :] = total
    group = lax.broadcasted_iota(I32, (ROWS, 128), 1) % 64 // 8
    result = jnp.zeros((ROWS, 128), F32)
    for j in range(2 * REACH + 1):
        start = edge + half * (j - REACH)
        result = jnp.where(group == j, padded[start : start + ROWS, :], result)
    out[...] = result


def reach_of(rows_beyond):
    return -(-rows_beyond // CX)


def widen_courant(pieces, wide, me):
    wide[MID : MID + BLK, :] = pieces[0][...].reshape(BLK, CZ)
    for k in range(1, REACH + 1):
        rows = 20 * CY - 16 * CY if k == REACH else BLK
        below, above = pieces[2 * k - 1], pieces[2 * k]
        has_below = jnp.where(me >= k, 1.0, 0.0)
        has_above = jnp.where(me + k < PEERS, 1.0, 0.0)
        wide[MID - (k - 1) * BLK - rows : MID - (k - 1) * BLK, :] = below[...].reshape(rows, CZ) * has_below
        wide[MID + k * BLK : MID + k * BLK + rows, :] = above[...].reshape(rows, CZ) * has_above


def laplace(bands, high, low, slot, start):
    xy_hi, xy_lo, z_hi, z_lo = bands
    window = pl.ds(pl.multiple_of(start - 64, 64), 256)
    centre = pl.ds(pl.multiple_of(start, 64), BLK)
    v_hi, v_lo = high[slot, window, :], low[slot, window, :]
    c_hi, c_lo = high[slot, centre, :], low[slot, centre, :]
    out = dot(xy_hi[...], v_hi) + dot(xy_lo[...], v_hi) + dot(xy_hi[...], v_lo)
    return out + dot(c_hi, z_hi[...]) + dot(c_lo, z_hi[...]) + dot(c_hi, z_lo[...])


def forward_kernel(*refs):
    pieces, refs = refs[:7], refs[7:]
    wavelet, owner, cell, *bands = refs[:7]
    drive = refs[7]
    wide, field_a, field_b, high, low, sources, change = refs[8:]
    me = lax.axis_index("space")
    widen_courant(pieces, wide, me)
    cells = cell[...]
    line = (owner[...] - me + REACH) * BLK + (cells >> 8)
    hot_z = one_hot(cells & 255, CZ)
    reaches = [reach_of(24 - 4 * t) for t in range(STEPS)]
    bases, at = [], 0
    for t in range(STEPS):
        bases.append(at - (REACH - reaches[t]) * BLK)
        at += (2 * reaches[t] + 1) * BLK
    amounts = [split2(wavelet[t]) for t in range(STEPS)]
    for block in range(2 * REACH + 1):
        mask = one_hot(line, BLK, block * BLK)
        for t in range(STEPS):
            if abs(block - REACH) <= reaches[t]:
                hi, lo = amounts[t]
                value = dot_nt(mask * hi, hot_z) + dot_nt(mask * lo, hot_z)
                sources[bases[t] + block * BLK : bases[t] + (block + 1) * BLK, :] = value
    fields = (field_a, field_b)
    start = sources[0:EXT, :]
    field_a[...] = start
    field_b[...] = jnp.zeros((EXT, CZ), F32)
    hi, lo = split2(start)
    high[0], low[0] = hi, lo
    for t in range(1, STEPS):
        now, other = fields[(t - 1) % 2], fields[t % 2]
        slot = (t - 1) % 2
        beyond = 24 - 4 * t
        first = MID - beyond * CY

        def chunk(i, carry, now=now, other=other, slot=slot, first=first, t=t):
            begin = pl.multiple_of(first + i * BLK, 64)
            at = pl.ds(begin, BLK)
            step = wide[at, :] * laplace(bands, high, low, slot, begin)
            step = step + sources[pl.ds(pl.multiple_of(bases[t] + begin, 64), BLK), :]
            change[at, :] = step
            new = (2.0 * now[at, :] - other[at, :]) + step
            other[at, :] = new
            hi, lo = split2(new)
            high[1 - slot, at, :], low[1 - slot, at, :] = hi, lo
            return carry

        lax.fori_loop(0, 2 * (beyond // CX) + 1 + (1 if beyond % CX else 0), chunk, 0)
        drive[t - 1] = change[MID : MID + BLK, :]


def adjoint_kernel(*refs):
    pieces, refs = refs[:7], refs[7:]
    got, drive, *bands = refs[:6]
    keep, send = refs[6:8]
    wide, field_a, field_b, high, low, stations, total = refs[8:]
    me = lax.axis_index("space")
    member = lax.axis_index("batch")
    widen_courant(pieces, wide, me)
    wide[0 : 64, :] = jnp.zeros((64, CZ), F32)
    wide[EXT - 64 : EXT, :] = jnp.zeros((64, CZ), F32)
    slots = got[...].T
    reaches = {t: reach_of(4 * (t - 1)) for t in range(1, STEPS)}
    bases, at = {}, 0
    for t in range(1, STEPS):
        bases[t] = at - (REACH - reaches[t]) * BLK
        at += (2 * reaches[t] + 1) * BLK
    for block in range(2 * REACH + 1):
        words = jnp.concatenate(
            [slots[block * 8 : block * 8 + 8, :], slots[64 + block * 8 : 72 + block * 8, :]], axis=1
        )
        cells = words[6:7, :].astype(I32)
        mask = one_hot(cells >> 8, BLK)
        hot_z = one_hot(cells & 255, CZ)
        for t in range(1, STEPS):
            if abs(block - REACH) <= reaches[t]:
                hi, lo = split2(words[t - 1 : t, :])
                value = dot_nt(mask * hi, hot_z) + dot_nt(mask * lo, hot_z)
                stations[bases[t] + block * BLK : bases[t] + (block + 1) * BLK, :] = value
    fields = (field_a, field_b)
    start = stations[bases[6] : bases[6] + EXT, :]
    field_a[...] = start
    field_b[...] = jnp.zeros((EXT, CZ), F32)
    hi, lo = split2(start * wide[...])
    high[0], low[0] = hi, lo
    total[...] = field_a[MID : MID + BLK, :] * drive[5]
    for t in range(STEPS - 2, 0, -1):
        n = STEPS - 2 - t
        now, other = fields[n % 2], fields[(n + 1) % 2]
        slot = n % 2
        beyond = 4 * (t - 1)
        first = MID - beyond * CY

        def chunk(i, carry, now=now, other=other, slot=slot, first=first, t=t):
            begin = pl.multiple_of(first + i * BLK, 64)
            at = pl.ds(begin, BLK)
            new = laplace(bands, high, low, slot, begin)
            new = new + stations[pl.ds(pl.multiple_of(bases[t] + begin, 64), BLK), :]
            new = (2.0 * now[at, :] - other[at, :]) + new
            other[at, :] = new
            hi, lo = split2(new * wide[at, :])
            high[1 - slot, at, :], low[1 - slot, at, :] = hi, lo
            return carry

        lax.fori_loop(0, 2 * (beyond // CX) + 1 + (1 if beyond % CX else 0), chunk, 0)
        total[...] += other[MID : MID + BLK, :] * drive[t - 1]
    gradient = total[...].reshape(CX, CY, CZ)
    squares = jnp.sum(jnp.sum(gradient * gradient, axis=0), axis=0, keepdims=True)
    norm = jnp.sum(squares, axis=1, keepdims=True)
    front, back = gradient[:, 0:8, :], gradient[:, 8:16, :]
    keep[0:CX] = jnp.where(member == 0, front, back)
    send[0:CX] = jnp.where(member == 0, back, front)
    keep[CX] = jnp.broadcast_to(norm, (8, CZ))
    send[CX] = jnp.broadcast_to(norm, (8, CZ))


def finish_kernel(keep, other, norms, update, share):
    sums = jnp.sum(norms[...], axis=0, keepdims=True)
    cells = float(PEERS * BLK * CZ)
    mean_first = sums[0:1, 0:1] / cells
    mean_second = sums[0:1, 64:65] / cells
    scale = jnp.sqrt((mean_first + mean_second) / 2.0 + epsilon)
    update[...] = (keep[0:CX] + other[0:CX]) / scale.reshape(1, 1, 1)
    ratio = (mean_first + epsilon) / (mean_first + mean_second + 2.0 * epsilon)
    share[...] = jnp.broadcast_to(ratio, (1, 128))


VM = pl.BlockSpec(memory_space=pltpu.VMEM)


def call(kernel, outs, scratch, *args, flops=0, limit=None):
    size = sum(int(np.prod(a.shape)) * 4 for a in args)
    return pl.pallas_call(
        kernel,
        out_shape=outs,
        in_specs=[VM] * len(args),
        out_specs=jax.tree.map(lambda _: VM, outs),
        scratch_shapes=scratch,
        cost_estimate=pl.CostEstimate(flops=flops, bytes_accessed=size, transcendentals=0),
    )(*args)


def shape(*dims, dtype=F32):
    return jax.ShapeDtypeStruct(dims, dtype)


def body(courant, wavelet, source_owner, source_cell, traces, station_owner, station_cell):
    def shift(value, k):
        return lax.ppermute(value, "space", [(i, (i + k) % PEERS) for i in range(PEERS)])

    pieces = [courant]
    for k in range(1, REACH + 1):
        below, above = (courant[4:], courant[:4]) if k == REACH else (courant, courant)
        pieces += [shift(below, k), shift(above, -k)]
    sent = call(
        prep_kernel,
        shape(ROWS, 128),
        [pltpu.VMEM((8, ROWS), F32), pltpu.VMEM((ROWS + 32, 128), F32)],
        jnp.transpose(traces, (2, 0, 1)),
        station_owner.reshape(1, ROWS),
        station_cell,
        flops=10**8,
    )
    got = lax.all_to_all(sent.reshape(PEERS, 4, 128), "space", split_axis=0, concat_axis=0, tiled=True)
    bands = [jnp.asarray(b) for b in taps()]
    fields = [pltpu.VMEM((EXT, CZ), F32)] * 3 + [pltpu.VMEM((2, EXT, CZ), BF16)] * 2
    drive = call(
        forward_kernel,
        shape(STEPS - 1, BLK, CZ),
        fields + [pltpu.VMEM((31 * BLK, CZ), F32), pltpu.VMEM((EXT, CZ), F32)],
        *pieces,
        jnp.transpose(wavelet, (2, 0, 1)),
        source_owner,
        source_cell,
        *bands,
        flops=4 * 10**9,
    )
    keep, send = call(
        adjoint_kernel,
        (shape(CX + 1, 8, CZ), shape(CX + 1, 8, CZ)),
        fields + [pltpu.VMEM((24 * BLK, CZ), F32), pltpu.VMEM((BLK, CZ), F32)],
        *pieces,
        got.reshape(ROWS, 128),
        drive,
        *bands,
        flops=4 * 10**9,
    )
    other = lax.ppermute(send, "batch", [(0, 1), (1, 0)])
    mine, theirs = keep[CX, 0, 0], other[CX, 0, 0]
    first = lax.axis_index("batch") == 0
    lanes = lax.broadcasted_iota(I32, (PEERS, 128), 1) < 64
    partial = jnp.where(lanes == first, mine, theirs)
    norms = lax.all_to_all(partial, "space", split_axis=0, concat_axis=0, tiled=True)
    update, share = call(
        finish_kernel, (shape(CX, 8, CZ), shape(1, 128)), [], keep, other, norms.reshape(PEERS, 128)
    )
    return update, share[0, 0:1]


def solution(mesh):
    placed = (
        P("space", None, None),
        P("batch", None, None),
        P("batch", None),
        P("batch", None),
        P("batch", "space", None),
        P("batch", "space", None),
        P("batch", "space"),
    )
    return jax.shard_map(
        body,
        mesh=mesh,
        in_specs=placed,
        out_specs=(P("space", "batch", None), P()),
        check_vma=False,
    )
```

```python
import jax
import jax.numpy as jnp
import numpy as np
from jax import lax
from jax.experimental import pallas as pl
from jax.experimental.pallas import tpu as pltpu
from jax.sharding import PartitionSpec as P

F32, BF16, I32 = jnp.float32, jnp.bfloat16, jnp.int32
center_tap = -205.0 / 72.0
stencil_taps = (1.6, -0.2, 8.0 / 315.0, -1.0 / 560.0)
epsilon = 1e-06

CX, CY, CZ = 8, 16, 256
BLK = CX * CY
REACH = 3
EXT = (2 * REACH + 1) * BLK
MID = REACH * BLK
WIDE = (2 * REACH + 1) * CX
STEPS = 7
SRC = 256
ROWS = 256
SLOTS = 8
PEERS = 64


def split2(x):
    hi = x.astype(BF16)
    return hi, (x - hi.astype(F32)).astype(BF16)


SCALE = 1.6 / 63.0
TAPS = (63.0, -7.875, 1.0, -9.0 / 128.0)
CENTRE_XY, CENTRE_Z = -336.0, -21.0 / 64.0


def band_z():
    band = np.zeros((CZ, CZ), np.float64)
    for z in range(CZ):
        band[z, z] = CENTRE_Z
        for k in range(1, 5):
            for other in (z + k, z - k):
                if 0 <= other < CZ:
                    band[other, z] = TAPS[k - 1]
    return band.astype(jnp.bfloat16)


def dot(a, b):
    return lax.dot_general(a, b, (((1,), (0,)), ((), ())), preferred_element_type=F32)


def dot_nt(a, b):
    return lax.dot_general(a, b, (((1,), (1,)), ((), ())), preferred_element_type=F32)


def one_hot(index_row, height, base=0):
    iota = lax.broadcasted_iota(I32, (height, index_row.shape[1]), 0) + base
    return jnp.where(iota == index_row, 1.0, 0.0).astype(BF16)


def prep_kernel(traces, owner, cell, courant, out, front, back, words, padded):
    front[...] = courant[0 : CX // 2]
    back[...] = courant[CX // 2 :]
    own = owner[...]
    own_f = own.astype(F32)
    column = jnp.broadcast_to(own_f, (128, ROWS)).T
    column = jnp.concatenate([column, column], axis=1)
    first = lax.broadcasted_iota(I32, (ROWS, ROWS), 0)
    second = lax.broadcasted_iota(I32, (ROWS, ROWS), 1)
    same = (column == jnp.broadcast_to(own_f, (ROWS, ROWS))) & (first < second)
    rank = jnp.sum(jnp.where(same, 1.0, 0.0), axis=0, keepdims=True).astype(I32)
    half = SLOTS // 2
    low = rank < half
    place = own * half + jnp.where(low, rank, rank - half)
    hot_low = one_hot(jnp.where(low, place, -1), PEERS * half)
    hot_high = one_hot(jnp.where(low, -1, place), PEERS * half)
    hot = jnp.concatenate([hot_low, hot_high], axis=1)
    for t in range(1, STEPS):
        words[t - 1 : t, :] = traces[t]
    words[6:7, :] = cell[...].astype(F32)
    words[7:8, :] = jnp.zeros((1, ROWS), F32)
    rest = words[...]
    total = None
    for _ in range(3):
        piece = rest.astype(BF16)
        rest = rest - piece.astype(F32)
        wide = jnp.concatenate([piece.astype(F32)] * 8, axis=0)
        empty = jnp.zeros_like(wide)
        both = jnp.concatenate(
            [jnp.concatenate([wide, empty], axis=1), jnp.concatenate([empty, wide], axis=1)], axis=0
        ).astype(BF16)
        part = dot_nt(hot, both)
        total = part if total is None else total + part
    edge = 16
    padded[0:edge, :] = jnp.zeros((edge, 128), F32)
    padded[edge + ROWS : edge + ROWS + edge, :] = jnp.zeros((edge, 128), F32)
    padded[edge : edge + ROWS, :] = total
    group = lax.broadcasted_iota(I32, (ROWS, 128), 1) % 64 // 8
    result = jnp.zeros((ROWS, 128), F32)
    for j in range(2 * REACH + 1):
        start = edge + half * (j - REACH)
        result = jnp.where(group == j, padded[start : start + ROWS, :], result)
    out[...] = result


def widen_courant(pieces, wide, me):
    wide[0:64, :] = jnp.zeros((64, CZ), F32)
    wide[EXT - 64 : EXT, :] = jnp.zeros((64, CZ), F32)
    wide[MID : MID + BLK, :] = pieces[0][...].reshape(BLK, CZ) * SCALE
    for k in range(1, REACH + 1):
        rows = BLK // 2 if k == REACH else BLK
        below, above = pieces[2 * k - 1], pieces[2 * k]
        has_below = jnp.where(me >= k, SCALE, 0.0)
        has_above = jnp.where(me + k < PEERS, SCALE, 0.0)
        wide[MID - (k - 1) * BLK - rows : MID - (k - 1) * BLK, :] = below[...].reshape(rows, CZ) * has_below
        wide[MID + k * BLK : MID + k * BLK + rows, :] = above[...].reshape(rows, CZ) * has_above


def clear_rims(field):
    rim = jnp.zeros((WIDE, 2, 8, 128), F32)
    field[:, :, 0:8, :] = rim
    field[:, :, 24:32, :] = rim


def laplace_xy(field, x, half):
    centre = field[pl.ds(x, CX), half, 8:24, :]
    out = CENTRE_XY * centre
    for k in range(1, 5):
        pairs = field[pl.ds(x + k, CX), half, 8:24, :] + field[pl.ds(x - k, CX), half, 8:24, :]
        pairs = pairs + field[pl.ds(x, CX), half, 8 + k : 24 + k, :]
        pairs = pairs + field[pl.ds(x, CX), half, 8 - k : 24 - k, :]
        out = out + TAPS[k - 1] * pairs
    return out


def rows_at(x, base=0):
    return pl.ds(pl.multiple_of(base + x * CY, 64), BLK)


def store_split(high, low, slot, x, half, value):
    hi, lo = split2(value.reshape(BLK, 128))
    at = rows_at(x)
    lanes = slice(half * 128, half * 128 + 128)
    high[slot, at, lanes], low[slot, at, lanes] = hi, lo


def over_chunks(beyond, chunk):
    def step(i, carry):
        chunk(REACH * CX - beyond + CX * i)
        return carry

    lax.fori_loop(0, beyond // 4 + 1, step, 0)


def field_kernel(*refs):
    pieces, refs = refs[:7], refs[7:]
    wavelet, owner, cell, got, band = refs[:5]
    keep, send, norms = refs[5:8]
    wide, rim_a, rim_b, field_a, field_b, high, low, masks, sources, stations, drive, total, part = refs[8:]
    me = lax.axis_index("space")
    member = lax.axis_index("batch")
    halves = [slice(0, 128), slice(128, 256)]

    def along(slot, x):
        at = rows_at(x)
        return dot(high[slot, at, :], band[...]) + dot(low[slot, at, :], band[...])

    cells = cell[...]
    line = (owner[...] - me + REACH) * BLK + (cells >> 8)
    hot_z = one_hot(cells & 255, CZ)
    for block in range(2 * REACH + 1):
        masks[block * BLK : (block + 1) * BLK, :] = one_hot(line, BLK, block * BLK)
    bases, at = [], 0
    for t in range(STEPS):
        reach = 24 - 4 * t
        rows = (2 * reach + CX) * CY
        first = MID - reach * CY
        bases.append(at - first)
        hi, lo = split2(wavelet[t])
        mask = masks[first : first + rows, :]
        sources[at : at + rows, :] = dot_nt(mask * hi, hot_z) + dot_nt(mask * lo, hot_z)
        at += rows
    widen_courant(pieces, wide, me)
    clear_rims(rim_a)
    clear_rims(rim_b)
    rims = (rim_a, rim_b)

    def begin(x):
        for half, lanes in enumerate(halves):
            value = sources[rows_at(x), lanes].reshape(CX, CY, 128)
            rim_a[pl.ds(x, CX), half, 8:24, :] = value
            store_split(high, low, 0, x, half, value)

    over_chunks(24, begin)
    for t in range(1, STEPS):
        now, other, slot = rims[(t - 1) % 2], rims[t % 2], (t - 1) % 2

        def chunk(x, now=now, other=other, slot=slot, t=t):
            at = rows_at(x)
            z_part = along(slot, x)
            for half in range(2):
                part[half] = laplace_xy(now, x, half)
            for half, lanes in enumerate(halves):
                lap = part[half] + z_part[:, lanes].reshape(CX, CY, 128)
                step = wide[at, lanes].reshape(CX, CY, 128) * lap
                step = step + sources[rows_at(x, bases[t]), lanes].reshape(CX, CY, 128)
                drive[t - 1, at, lanes] = step.reshape(BLK, 128)
                if t < STEPS - 1:
                    new = 2.0 * now[pl.ds(x, CX), half, 8:24, :] + step
                    if t > 1:
                        new = new - other[pl.ds(x, CX), half, 8:24, :]
                    other[pl.ds(x, CX), half, 8:24, :] = new
                    store_split(high, low, 1 - slot, x, half, new)

        over_chunks(24 - 4 * t, chunk)

    slots = got[...].T
    spans, bases, at = {}, {}, 0
    for t in range(1, STEPS):
        reach = 4 * (t - 1)
        spans[t] = (MID - reach * CY, MID + BLK + reach * CY)
        bases[t] = at - spans[t][0]
        at += spans[t][1] - spans[t][0]
    for block in range(2 * REACH + 1):
        words = jnp.concatenate(
            [slots[block * 8 : block * 8 + 8, :], slots[64 + block * 8 : 72 + block * 8, :]], axis=1
        )
        cells = words[6:7, :].astype(I32)
        mask = one_hot(cells >> 8, BLK)
        hot_z = one_hot(cells & 255, CZ)
        places, his, los = [], [], []
        for t in range(1, STEPS):
            lower = max(spans[t][0], block * BLK)
            upper = min(spans[t][1], block * BLK + BLK)
            if lower < upper:
                hi, lo = split2(words[t - 1 : t, :])
                wanted = mask[lower - block * BLK : upper - block * BLK]
                places.append((bases[t] + lower, upper - lower))
                his.append(wanted * hi)
                los.append(wanted * lo)
        value = dot_nt(jnp.concatenate(his, axis=0), hot_z) + dot_nt(jnp.concatenate(los, axis=0), hot_z)
        at = 0
        for place, rows in places:
            stations[place : place + rows, :] = value[at : at + rows]
            at += rows
    fields = (field_a, field_b)

    def begin_back(x):
        at = rows_at(x)
        for half, lanes in enumerate(halves):
            value = stations[rows_at(x, bases[6]), lanes].reshape(CX, CY, 128)
            field_a[pl.ds(x, CX), half] = value
            value = value * wide[at, lanes].reshape(CX, CY, 128)
            rim_a[pl.ds(x, CX), half, 8:24, :] = value
            store_split(high, low, 0, x, half, value)

    over_chunks(20, begin_back)

    def gather(field, t, first):
        for half, lanes in enumerate(halves):
            term = field[REACH * CX : REACH * CX + CX, half].reshape(BLK, 128)
            term = term * drive[t - 1, MID : MID + BLK, lanes]
            total[:, lanes] = term if first else total[:, lanes] + term

    gather(field_a, 6, True)
    for t in range(STEPS - 2, 0, -1):
        n = STEPS - 2 - t
        now, other, slot = fields[n % 2], fields[(n + 1) % 2], n % 2
        source, target = rims[slot], rims[1 - slot]

        def chunk(x, now=now, other=other, slot=slot, source=source, target=target, t=t, n=n):
            at = rows_at(x)
            z_part = along(slot, x)
            for half in range(2):
                part[half] = laplace_xy(source, x, half)
            for half, lanes in enumerate(halves):
                new = part[half] + z_part[:, lanes].reshape(CX, CY, 128)
                new = new + stations[rows_at(x, bases[t]), lanes].reshape(CX, CY, 128)
                new = new + 2.0 * now[pl.ds(x, CX), half]
                if n > 0:
                    new = new - other[pl.ds(x, CX), half]
                other[pl.ds(x, CX), half] = new
                if t > 1:
                    new = new * wide[at, lanes].reshape(CX, CY, 128)
                    target[pl.ds(x, CX), half, 8:24, :] = new
                    store_split(high, low, 1 - slot, x, half, new)

        over_chunks(4 * (t - 1), chunk)
        gather(other, t, False)
    gradient = total[...].reshape(CX, CY, CZ)
    squares = jnp.sum(jnp.sum(gradient * gradient, axis=0), axis=0, keepdims=True)
    norm = jnp.sum(squares, axis=1, keepdims=True)
    front, back = gradient[:, 0:8, :], gradient[:, 8:16, :]
    keep[...] = jnp.where(member == 0, front, back)
    send[...] = jnp.where(member == 0, back, front)
    norms[...] = jnp.broadcast_to(norm, (8, 128))


def finish_kernel(keep, other, norms, update, share):
    sums = jnp.sum(norms[...], axis=0, keepdims=True)
    cells = float(PEERS * BLK * CZ)
    mean_first = sums[0:1, 0:1] / cells
    mean_second = sums[0:1, 64:65] / cells
    scale = jnp.sqrt((mean_first + mean_second) / 2.0 + epsilon)
    update[...] = (keep[...] + other[...]) / scale.reshape(1, 1, 1)
    ratio = (mean_first + epsilon) / (mean_first + mean_second + 2.0 * epsilon)
    share[...] = jnp.broadcast_to(ratio, (1, 128))


VM = pl.BlockSpec(memory_space=pltpu.VMEM)


def call(kernel, outs, scratch, *args, flops=0, limit=4 << 20):
    size = sum(int(np.prod(a.shape)) * 4 for a in args)
    return pl.pallas_call(
        kernel,
        out_shape=outs,
        in_specs=[VM] * len(args),
        out_specs=jax.tree.map(lambda _: VM, outs),
        scratch_shapes=scratch,
        cost_estimate=pl.CostEstimate(flops=flops, bytes_accessed=size, transcendentals=0),
        compiler_params=pltpu.CompilerParams(vmem_limit_bytes=limit),
    )(*args)


def shape(*dims, dtype=F32):
    return jax.ShapeDtypeStruct(dims, dtype)


def body(courant, wavelet, source_owner, source_cell, traces, station_owner, station_cell):
    def shift(value, k):
        return lax.ppermute(value, "space", [(i, (i + k) % PEERS) for i in range(PEERS)])

    half_slab = shape(CX // 2, CY, CZ)
    sent, front, back = call(
        prep_kernel,
        (shape(ROWS, 128), half_slab, half_slab),
        [pltpu.VMEM((8, ROWS), F32), pltpu.VMEM((ROWS + 32, 128), F32)],
        jnp.transpose(traces, (2, 0, 1)),
        station_owner.reshape(1, ROWS),
        station_cell,
        courant,
        flops=10**8,
    )
    pieces = [courant]
    for k in range(1, REACH + 1):
        below, above = (back, front) if k == REACH else (courant, courant)
        pieces += [shift(below, k), shift(above, -k)]
    got = lax.all_to_all(sent.reshape(PEERS, 4, 128), "space", split_axis=0, concat_axis=0, tiled=True)
    keep, send, mine = call(
        field_kernel,
        (shape(CX, 8, CZ), shape(CX, 8, CZ), shape(8, 128)),
        [pltpu.VMEM((EXT, CZ), F32)]
        + [pltpu.VMEM((WIDE, 2, 32, 128), F32)] * 2
        + [pltpu.VMEM((WIDE, 2, CY, 128), F32)] * 2
        + [pltpu.VMEM((2, EXT, CZ), BF16)] * 2
        + [pltpu.VMEM((EXT, CZ), BF16)]
        + [pltpu.VMEM((28 * BLK, CZ), F32), pltpu.VMEM((21 * BLK, CZ), F32)]
        + [pltpu.VMEM((STEPS - 1, EXT, CZ), F32), pltpu.VMEM((BLK, CZ), F32)]
        + [pltpu.VMEM((2, CX, CY, 128), F32)],
        *pieces,
        jnp.transpose(wavelet, (2, 0, 1)),
        source_owner,
        source_cell,
        got.reshape(ROWS, 128),
        jnp.asarray(band_z()),
        flops=8 * 10**9,
        limit=30 << 20,
    )
    swap = [(0, 1), (1, 0)]
    theirs = lax.ppermute(mine, "batch", swap)
    other = lax.ppermute(send, "batch", swap)
    lanes = lax.broadcasted_iota(I32, (8, 128), 1) < 64
    row = jnp.where(lanes == (lax.axis_index("batch") == 0), mine, theirs)
    partial = jnp.broadcast_to(row[0:1][None], (PEERS, 1, 128))
    norms = lax.all_to_all(partial, "space", split_axis=0, concat_axis=0, tiled=True)
    update, share = call(
        finish_kernel, (shape(CX, 8, CZ), shape(1, 128)), [], keep, other, norms.reshape(PEERS, 128)
    )
    return update, share[0, 0:1]


def solution(mesh):
    placed = (
        P("space", None, None),
        P("batch", None, None),
        P("batch", None),
        P("batch", None),
        P("batch", "space", None),
        P("batch", "space", None),
        P("batch", "space"),
    )
    return jax.shard_map(
        body,
        mesh=mesh,
        in_specs=placed,
        out_specs=(P("space", "batch", None), P()),
        check_vma=False,
    )
```

```python
import jax
import jax.numpy as jnp
import numpy as np
from jax import lax
from jax.experimental import pallas as pl
from jax.experimental.pallas import tpu as pltpu
from jax.sharding import PartitionSpec as P


F32, BF16, I32 = jnp.float32, jnp.bfloat16, jnp.int32
epsilon = 1e-06

CX, CY, CZ = 8, 16, 256
BLK = CX * CY
REACH = 3
EXT = (2 * REACH + 1) * BLK
MID = REACH * BLK
WIDE = (2 * REACH + 1) * CX
STEPS = 7
ROWS = 256
SLOTS = 8
PEERS = 64


def split2(x):
    hi = x.astype(BF16)
    return hi, (x - hi.astype(F32)).astype(BF16)


SCALE = 1.6 / 63.0
TAPS = (63.0, -7.875, 1.0, -9.0 / 128.0)
CENTRE_XY, CENTRE_Z = -336.0, -21.0 / 64.0


def band_z():
    band = np.zeros((CZ, CZ), np.float64)
    for z in range(CZ):
        band[z, z] = CENTRE_Z
        for k in range(1, 5):
            for other in (z + k, z - k):
                if 0 <= other < CZ:
                    band[other, z] = TAPS[k - 1]
    return band.astype(jnp.bfloat16)


def dot(a, b):
    return lax.dot_general(a, b, (((1,), (0,)), ((), ())), preferred_element_type=F32)


def dot_nt(a, b):
    return lax.dot_general(a, b, (((1,), (1,)), ((), ())), preferred_element_type=F32)


def one_hot(index_row, height, base=0):
    iota = lax.broadcasted_iota(I32, (height, index_row.shape[1]), 0) + base
    return jnp.where(iota == index_row, 1.0, 0.0).astype(BF16)


TRACES, WAVELET, OWNER, CELL, SOURCE_OWNER, SOURCE_CELL, TABLE = 0, 7, 14, 15, 16, 17, 24


def prep_kernel(table, out, words, padded):
    own_f = table[OWNER : OWNER + 1]
    own = own_f.astype(I32)
    column = jnp.broadcast_to(own_f, (128, ROWS)).T
    column = jnp.concatenate([column, column], axis=1)
    first = lax.broadcasted_iota(I32, (ROWS, ROWS), 0)
    second = lax.broadcasted_iota(I32, (ROWS, ROWS), 1)
    same = (column == jnp.broadcast_to(own_f, (ROWS, ROWS))) & (first < second)
    rank = jnp.sum(jnp.where(same, 1.0, 0.0), axis=0, keepdims=True).astype(I32)
    half = SLOTS // 2
    low = rank < half
    place = own * half + jnp.where(low, rank, rank - half)
    hot_low = one_hot(jnp.where(low, place, -1), PEERS * half)
    hot_high = one_hot(jnp.where(low, -1, place), PEERS * half)
    hot = jnp.concatenate([hot_low, hot_high], axis=1)
    for t in range(1, STEPS):
        words[t - 1 : t, :] = table[TRACES + t : TRACES + t + 1]
    words[6:7, :] = table[CELL : CELL + 1]
    words[7:8, :] = jnp.zeros((1, ROWS), F32)
    rest = words[...]
    total = None
    for _ in range(3):
        piece = rest.astype(BF16)
        rest = rest - piece.astype(F32)
        wide = jnp.concatenate([piece.astype(F32)] * 8, axis=0)
        empty = jnp.zeros_like(wide)
        both = jnp.concatenate(
            [jnp.concatenate([wide, empty], axis=1), jnp.concatenate([empty, wide], axis=1)], axis=0
        ).astype(BF16)
        part = dot_nt(hot, both)
        total = part if total is None else total + part
    edge = 16
    padded[0:edge, :] = jnp.zeros((edge, 128), F32)
    padded[edge + ROWS : edge + ROWS + edge, :] = jnp.zeros((edge, 128), F32)
    padded[edge : edge + ROWS, :] = total
    group = lax.broadcasted_iota(I32, (ROWS, 128), 1) % 64 // 8
    result = jnp.zeros((ROWS, 128), F32)
    for j in range(2 * REACH + 1):
        start = edge + half * (j - REACH)
        result = jnp.where(group == j, padded[start : start + ROWS, :], result)
    out[...] = result


def widen_courant(pieces, wide, me):
    wide[0:64, :] = jnp.zeros((64, CZ), F32)
    wide[EXT - 64 : EXT, :] = jnp.zeros((64, CZ), F32)
    wide[MID : MID + BLK, :] = pieces[0][...].reshape(BLK, CZ)
    _, below, above, lower, upper = pieces

    def inside(k):
        return jnp.where((me + k >= 0) & (me + k < PEERS), 1.0, 0.0)

    half = BLK // 2
    wide[half:BLK, :] = lower[0 : CX // 2].reshape(half, CZ) * inside(-3)
    wide[BLK : 2 * BLK, :] = lower[CX // 2 :].reshape(BLK, CZ) * inside(-2)
    wide[2 * BLK : MID, :] = below[...].reshape(BLK, CZ) * (SCALE * inside(-1))
    wide[MID + BLK : MID + 2 * BLK, :] = above[...].reshape(BLK, CZ) * (SCALE * inside(1))
    wide[MID + 2 * BLK : MID + 3 * BLK, :] = upper[0:CX].reshape(BLK, CZ) * inside(2)
    wide[MID + 3 * BLK : MID + 3 * BLK + half, :] = upper[CX:].reshape(half, CZ) * inside(3)


def clear_rims(field):
    rim = jnp.zeros((WIDE, 2, 8, 128), F32)
    field[:, :, 0:8, :] = rim
    field[:, :, 24:32, :] = rim


def laplace_xy(field, x, half):
    centre = field[pl.ds(x, CX), half, 8:24, :]
    out = CENTRE_XY * centre
    for k in range(1, 5):
        pairs = field[pl.ds(x + k, CX), half, 8:24, :] + field[pl.ds(x - k, CX), half, 8:24, :]
        pairs = pairs + field[pl.ds(x, CX), half, 8 + k : 24 + k, :]
        pairs = pairs + field[pl.ds(x, CX), half, 8 - k : 24 - k, :]
        out = out + TAPS[k - 1] * pairs
    return out


def rows_at(x, base=0):
    return pl.ds(pl.multiple_of(base + x * CY, 64), BLK)


def store_split(high, low, slot, x, half, value):
    hi, lo = split2(value.reshape(BLK, 128))
    at = rows_at(x)
    lanes = slice(half * 128, half * 128 + 128)
    high[slot, at, lanes], low[slot, at, lanes] = hi, lo


def over_chunks(beyond, chunk):
    def step(i, carry):
        chunk(REACH * CX - beyond + CX * i)
        return carry

    lax.fori_loop(0, beyond // 4 + 1, step, 0)


def join_kernel(courant, below, above, lower, upper):
    lower[0 : CX // 2] = below[CX // 2 :] * SCALE
    lower[CX // 2 :] = courant[...]
    upper[0:CX] = courant[...]
    upper[CX:] = above[0 : CX // 2] * SCALE


def source_places():
    bases, at = [], 0
    for t in range(STEPS):
        reach = 24 - 4 * t
        bases.append(at - (MID - reach * CY))
        at += (2 * reach + CX) * CY
    return bases


def station_places():
    spans, bases, at = {}, {}, 0
    for t in range(1, STEPS):
        reach = 4 * (t - 1)
        spans[t] = (MID - reach * CY, MID + BLK + reach * CY)
        bases[t] = at - spans[t][0]
        at += spans[t][1] - spans[t][0]
    return spans, bases


def inject_kernel(table, got, sources, stations, masks):
    me = lax.axis_index("space")
    cells = table[SOURCE_CELL : SOURCE_CELL + 1].astype(I32)
    line = (table[SOURCE_OWNER : SOURCE_OWNER + 1].astype(I32) - me + REACH) * BLK + (cells >> 8)
    hot_z = one_hot(cells & 255, CZ)
    for block in range(2 * REACH + 1):
        masks[block * BLK : (block + 1) * BLK, :] = one_hot(line, BLK, block * BLK)
    bases = source_places()
    for t in range(STEPS):
        reach = 24 - 4 * t
        rows = (2 * reach + CX) * CY
        first = MID - reach * CY
        at = bases[t] + first
        hi, lo = split2(table[WAVELET + t : WAVELET + t + 1])
        mask = masks[first : first + rows, :]
        sources[at : at + rows, :] = dot_nt(mask * hi, hot_z) + dot_nt(mask * lo, hot_z)
    slots = got[...].T
    spans, bases = station_places()
    for block in range(2 * REACH + 1):
        words = jnp.concatenate(
            [slots[block * 8 : block * 8 + 8, :], slots[64 + block * 8 : 72 + block * 8, :]], axis=1
        )
        cells = words[6:7, :].astype(I32)
        mask = one_hot(cells >> 8, BLK)
        hot_z = one_hot(cells & 255, CZ)
        places, his, los = [], [], []
        for t in range(1, STEPS):
            lower = max(spans[t][0], block * BLK)
            upper = min(spans[t][1], block * BLK + BLK)
            if lower < upper:
                hi, lo = split2(words[t - 1 : t, :])
                wanted = mask[lower - block * BLK : upper - block * BLK]
                places.append((bases[t] + lower, upper - lower))
                his.append(wanted * hi)
                los.append(wanted * lo)
        value = dot_nt(jnp.concatenate(his, axis=0), hot_z) + dot_nt(jnp.concatenate(los, axis=0), hot_z)
        at = 0
        for place, rows in places:
            stations[place : place + rows, :] = value[at : at + rows]
            at += rows


def field_kernel(*refs):
    pieces, refs = refs[:5], refs[5:]
    sources, stations, band = refs[:3]
    keep, send, norms = refs[3:6]
    wide, rim_a, rim_b, field_a, field_b, high, low, drive, total, part = refs[6:]
    me = lax.axis_index("space")
    member = lax.axis_index("batch")
    halves = [slice(0, 128), slice(128, 256)]

    def along(slot, x):
        at = rows_at(x)
        return dot(high[slot, at, :], band[...]) + dot(low[slot, at, :], band[...])

    bases = source_places()
    widen_courant(pieces, wide, me)
    clear_rims(rim_a)
    clear_rims(rim_b)
    rims = (rim_a, rim_b)

    def begin(x):
        for half, lanes in enumerate(halves):
            value = sources[rows_at(x), lanes].reshape(CX, CY, 128)
            rim_a[pl.ds(x, CX), half, 8:24, :] = value
            store_split(high, low, 0, x, half, value)

    over_chunks(24, begin)
    for t in range(1, STEPS):
        now, other, slot = rims[(t - 1) % 2], rims[t % 2], (t - 1) % 2

        def chunk(x, now=now, other=other, slot=slot, t=t):
            at = rows_at(x)
            z_part = along(slot, x)
            for half in range(2):
                part[half] = laplace_xy(now, x, half)
            for half, lanes in enumerate(halves):
                lap = part[half] + z_part[:, lanes].reshape(CX, CY, 128)
                step = wide[at, lanes].reshape(CX, CY, 128) * lap
                step = step + sources[rows_at(x, bases[t]), lanes].reshape(CX, CY, 128)
                drive[t - 1, at, lanes] = step.reshape(BLK, 128)
                if t < STEPS - 1:
                    new = 2.0 * now[pl.ds(x, CX), half, 8:24, :] + step
                    if t > 1:
                        new = new - other[pl.ds(x, CX), half, 8:24, :]
                    other[pl.ds(x, CX), half, 8:24, :] = new
                    store_split(high, low, 1 - slot, x, half, new)

        over_chunks(24 - 4 * t, chunk)

    _, bases = station_places()
    fields = (field_a, field_b)

    def begin_back(x):
        at = rows_at(x)
        for half, lanes in enumerate(halves):
            value = stations[rows_at(x, bases[6]), lanes].reshape(CX, CY, 128)
            field_a[pl.ds(x, CX), half] = value
            value = value * wide[at, lanes].reshape(CX, CY, 128)
            rim_a[pl.ds(x, CX), half, 8:24, :] = value
            store_split(high, low, 0, x, half, value)

    over_chunks(20, begin_back)

    def gather(field, t, first):
        for half, lanes in enumerate(halves):
            term = field[REACH * CX : REACH * CX + CX, half].reshape(BLK, 128)
            term = term * drive[t - 1, MID : MID + BLK, lanes]
            total[:, lanes] = term if first else total[:, lanes] + term

    gather(field_a, 6, True)
    for t in range(STEPS - 2, 0, -1):
        n = STEPS - 2 - t
        now, other, slot = fields[n % 2], fields[(n + 1) % 2], n % 2
        source, target = rims[slot], rims[1 - slot]

        def chunk(x, now=now, other=other, slot=slot, source=source, target=target, t=t, n=n):
            at = rows_at(x)
            z_part = along(slot, x)
            for half in range(2):
                part[half] = laplace_xy(source, x, half)
            for half, lanes in enumerate(halves):
                new = part[half] + z_part[:, lanes].reshape(CX, CY, 128)
                new = new + stations[rows_at(x, bases[t]), lanes].reshape(CX, CY, 128)
                new = new + 2.0 * now[pl.ds(x, CX), half]
                if n > 0:
                    new = new - other[pl.ds(x, CX), half]
                other[pl.ds(x, CX), half] = new
                if t > 1:
                    new = new * wide[at, lanes].reshape(CX, CY, 128)
                    target[pl.ds(x, CX), half, 8:24, :] = new
                    store_split(high, low, 1 - slot, x, half, new)

        over_chunks(4 * (t - 1), chunk)
        gather(other, t, False)
    gradient = total[...].reshape(CX, CY, CZ)
    squares = jnp.sum(jnp.sum(gradient * gradient, axis=0), axis=0, keepdims=True)
    norm = jnp.sum(squares, axis=1, keepdims=True)
    front, back = gradient[:, 0:8, :], gradient[:, 8:16, :]
    keep[...] = jnp.where(member == 0, front, back)
    send[...] = jnp.where(member == 0, back, front)
    norms[...] = jnp.broadcast_to(norm, (8, 128))


def finish_kernel(keep, other, norms, update, share):
    sums = jnp.sum(norms[...], axis=0, keepdims=True)
    cells = float(PEERS * BLK * CZ)
    mean_first = sums[0:1, 0:1] / cells
    mean_second = sums[0:1, 64:65] / cells
    scale = jnp.sqrt((mean_first + mean_second) / 2.0 + epsilon)
    update[...] = (keep[...] + other[...]) / scale.reshape(1, 1, 1)
    ratio = (mean_first + epsilon) / (mean_first + mean_second + 2.0 * epsilon)
    share[...] = jnp.broadcast_to(ratio, (1, 128))


VM = pl.BlockSpec(memory_space=pltpu.VMEM)


def call(kernel, outs, scratch, *args, flops=0, limit=4 << 20):
    size = sum(int(np.prod(a.shape)) * 4 for a in args)
    return pl.pallas_call(
        kernel,
        out_shape=outs,
        in_specs=[VM] * len(args),
        out_specs=jax.tree.map(lambda _: VM, outs),
        scratch_shapes=scratch,
        cost_estimate=pl.CostEstimate(flops=flops, bytes_accessed=size, transcendentals=0),
        compiler_params=pltpu.CompilerParams(vmem_limit_bytes=limit),
    )(*args)


def shape(*dims, dtype=F32):
    return jax.ShapeDtypeStruct(dims, dtype)


def body(courant, wavelet, source_owner, source_cell, traces, station_owner, station_cell):
    def shift(value, k):
        return lax.ppermute(value, "space", [(i, (i + k) % PEERS) for i in range(PEERS)])

    singles = [station_owner.reshape(1, ROWS), station_cell, source_owner, source_cell]
    table = [jnp.transpose(traces[0]), jnp.transpose(wavelet[0])] + [v.astype(F32) for v in singles]
    table = jnp.concatenate(table + [jnp.zeros((TABLE - 18, ROWS), F32)], axis=0)
    slab = courant * SCALE
    scratch = [pltpu.VMEM((8, ROWS), F32), pltpu.VMEM((ROWS + 32, 128), F32)]
    sent = call(prep_kernel, shape(ROWS, 128), scratch, table, flops=10**8)
    below, above = shift(courant, 1), shift(courant, -1)
    taller = shape(CX + CX // 2, CY, CZ)
    lower, upper = call(join_kernel, (taller, taller), [], slab, below, above)
    pieces = [slab, below, above, shift(lower, 2), shift(upper, -2)]
    got = lax.all_to_all(sent.reshape(PEERS, 4, 128), "space", split_axis=0, concat_axis=0, tiled=True)
    sources, stations = call(
        inject_kernel,
        (shape(28 * BLK, CZ), shape(21 * BLK, CZ)),
        [pltpu.VMEM((EXT, CZ), BF16)],
        table,
        got.reshape(ROWS, 128),
        flops=4 * 10**9,
        limit=12 << 20,
    )
    keep, send, mine = call(
        field_kernel,
        (shape(CX, 8, CZ), shape(CX, 8, CZ), shape(8, 128)),
        [pltpu.VMEM((EXT, CZ), F32)]
        + [pltpu.VMEM((WIDE, 2, 32, 128), F32)] * 2
        + [pltpu.VMEM((WIDE, 2, CY, 128), F32)] * 2
        + [pltpu.VMEM((2, EXT, CZ), BF16)] * 2
        + [pltpu.VMEM((STEPS - 1, EXT, CZ), F32), pltpu.VMEM((BLK, CZ), F32)]
        + [pltpu.VMEM((2, CX, CY, 128), F32)],
        *pieces,
        sources,
        stations,
        jnp.asarray(band_z()),
        flops=4 * 10**9,
        limit=30 << 20,
    )
    swap = [(0, 1), (1, 0)]
    theirs = lax.ppermute(mine, "batch", swap)
    other = lax.ppermute(send, "batch", swap)
    lanes = lax.broadcasted_iota(I32, (8, 128), 1) < 64
    row = jnp.where(lanes == (lax.axis_index("batch") == 0), mine, theirs)
    partial = jnp.broadcast_to(row[0:1][None], (PEERS, 1, 128))
    norms = lax.all_to_all(partial, "space", split_axis=0, concat_axis=0, tiled=True)
    update, share = call(
        finish_kernel, (shape(CX, 8, CZ), shape(1, 128)), [], keep, other, norms.reshape(PEERS, 128)
    )
    return update, share[0, 0:1]


def solution(mesh):
    placed = (
        P("space", None, None),
        P("batch", None, None),
        P("batch", None),
        P("batch", None),
        P("batch", "space", None),
        P("batch", "space", None),
        P("batch", "space"),
    )
    return jax.shard_map(
        body,
        mesh=mesh,
        in_specs=placed,
        out_specs=(P("space", "batch", None), P()),
        check_vma=False,
    )
```

```python
import jax
import jax.numpy as jnp
import numpy as np
from jax import lax
from jax.experimental import pallas as pl
from jax.experimental.pallas import tpu as pltpu
from jax.sharding import PartitionSpec as P


F32, BF16, I32 = jnp.float32, jnp.bfloat16, jnp.int32
epsilon = 1e-06

CX, CY, CZ = 8, 16, 256
BLK = CX * CY
REACH = 3
EXT = (2 * REACH + 1) * BLK
MID = REACH * BLK
WIDE = (2 * REACH + 1) * CX
STEPS = 7
ROWS = 256
SLOTS = 8
PEERS = 64


def split2(x):
    hi = x.astype(BF16)
    return hi, (x - hi.astype(F32)).astype(BF16)


SCALE = 1.6 / 63.0
TAPS = (63.0, -7.875, 1.0, -9.0 / 128.0)
CENTRE_XY, CENTRE_Z = -336.0, -21.0 / 64.0


def band_z():
    band = np.zeros((CZ, CZ), np.float64)
    for z in range(CZ):
        band[z, z] = CENTRE_Z
        for k in range(1, 5):
            for other in (z + k, z - k):
                if 0 <= other < CZ:
                    band[other, z] = TAPS[k - 1]
    return band.astype(jnp.bfloat16)


def dot(a, b):
    return lax.dot_general(a, b, (((1,), (0,)), ((), ())), preferred_element_type=F32)


def dot_nt(a, b):
    return lax.dot_general(a, b, (((1,), (1,)), ((), ())), preferred_element_type=F32)


def one_hot(index_row, height, base=0):
    iota = lax.broadcasted_iota(I32, (height, index_row.shape[1]), 0) + base
    return jnp.where(iota == index_row, 1.0, 0.0).astype(BF16)


def prep_kernel(traces, owner, cell, courant, out, front, back, words, padded):
    front[...] = courant[0 : CX // 2]
    back[...] = courant[CX // 2 :]
    own = owner[...]
    own_f = own.astype(F32)
    column = jnp.broadcast_to(own_f, (128, ROWS)).T
    column = jnp.concatenate([column, column], axis=1)
    first = lax.broadcasted_iota(I32, (ROWS, ROWS), 0)
    second = lax.broadcasted_iota(I32, (ROWS, ROWS), 1)
    same = (column == jnp.broadcast_to(own_f, (ROWS, ROWS))) & (first < second)
    rank = jnp.sum(jnp.where(same, 1.0, 0.0), axis=0, keepdims=True).astype(I32)
    half = SLOTS // 2
    low = rank < half
    place = own * half + jnp.where(low, rank, rank - half)
    hot_low = one_hot(jnp.where(low, place, -1), PEERS * half)
    hot_high = one_hot(jnp.where(low, -1, place), PEERS * half)
    hot = jnp.concatenate([hot_low, hot_high], axis=1)
    for t in range(1, STEPS):
        words[t - 1 : t, :] = traces[t]
    words[6:7, :] = cell[...].astype(F32)
    words[7:8, :] = jnp.zeros((1, ROWS), F32)
    rest = words[...]
    total = None
    for _ in range(3):
        piece = rest.astype(BF16)
        rest = rest - piece.astype(F32)
        wide = jnp.concatenate([piece.astype(F32)] * 8, axis=0)
        empty = jnp.zeros_like(wide)
        both = jnp.concatenate(
            [jnp.concatenate([wide, empty], axis=1), jnp.concatenate([empty, wide], axis=1)], axis=0
        ).astype(BF16)
        part = dot_nt(hot, both)
        total = part if total is None else total + part
    edge = 16
    padded[0:edge, :] = jnp.zeros((edge, 128), F32)
    padded[edge + ROWS : edge + ROWS + edge, :] = jnp.zeros((edge, 128), F32)
    padded[edge : edge + ROWS, :] = total
    group = lax.broadcasted_iota(I32, (ROWS, 128), 1) % 64 // 8
    result = jnp.zeros((ROWS, 128), F32)
    for j in range(2 * REACH + 1):
        start = edge + half * (j - REACH)
        result = jnp.where(group == j, padded[start : start + ROWS, :], result)
    out[...] = result


def widen_courant(pieces, wide, me):
    wide[0:64, :] = jnp.zeros((64, CZ), F32)
    wide[EXT - 64 : EXT, :] = jnp.zeros((64, CZ), F32)
    wide[MID : MID + BLK, :] = pieces[0][...].reshape(BLK, CZ) * SCALE
    for k in range(1, REACH + 1):
        rows = BLK // 2 if k == REACH else BLK
        below, above = pieces[2 * k - 1], pieces[2 * k]
        has_below = jnp.where(me >= k, SCALE, 0.0)
        has_above = jnp.where(me + k < PEERS, SCALE, 0.0)
        wide[MID - (k - 1) * BLK - rows : MID - (k - 1) * BLK, :] = below[...].reshape(rows, CZ) * has_below
        wide[MID + k * BLK : MID + k * BLK + rows, :] = above[...].reshape(rows, CZ) * has_above


def clear_rims(field):
    rim = jnp.zeros((WIDE, 2, 8, 128), F32)
    field[:, :, 0:8, :] = rim
    field[:, :, 24:32, :] = rim


def laplace_xy(field, x, half, rows):
    centre = field[pl.ds(x, rows), half, 8:24, :]
    out = CENTRE_XY * centre
    for k in range(1, 5):
        pairs = field[pl.ds(x + k, rows), half, 8:24, :] + field[pl.ds(x - k, rows), half, 8:24, :]
        pairs = pairs + field[pl.ds(x, rows), half, 8 + k : 24 + k, :]
        pairs = pairs + field[pl.ds(x, rows), half, 8 - k : 24 - k, :]
        out = out + TAPS[k - 1] * pairs
    return out


def rows_at(x, rows, base=0):
    return pl.ds(pl.multiple_of(base + x * CY, 64), rows * CY)


def store_split(high, low, slot, x, half, value, rows):
    hi, lo = split2(value.reshape(rows * CY, 128))
    at = rows_at(x, rows)
    lanes = slice(half * 128, half * 128 + 128)
    high[slot, at, lanes], low[slot, at, lanes] = hi, lo


TRIP = {56: 8, 48: 16, 40: 20, 32: 16, 24: 24, 16: 16, 8: 8}


def over_chunks(beyond, chunk):
    total = 2 * beyond + CX
    rows = TRIP[total]

    def step(i, carry):
        chunk(REACH * CX - beyond + rows * i, rows)
        return carry

    if rows == total:
        step(0, 0)
    else:
        lax.fori_loop(0, total // rows, step, 0)


def pieces_of(rows):
    return [(i, min(CX, rows - i)) for i in range(0, rows, CX)]


def source_places():
    bases, at = [], 0
    for t in range(STEPS):
        reach = 24 - 4 * t
        bases.append(at - (MID - reach * CY))
        at += (2 * reach + CX) * CY
    return bases


def station_places():
    spans, bases, at = {}, {}, 0
    for t in range(1, STEPS):
        reach = 4 * (t - 1)
        spans[t] = (MID - reach * CY, MID + BLK + reach * CY)
        bases[t] = at - spans[t][0]
        at += spans[t][1] - spans[t][0]
    return spans, bases


def inject_kernel(wavelet, owner, cell, got, sources, stations, masks):
    me = lax.axis_index("space")
    cells = cell[...]
    line = (owner[...] - me + REACH) * BLK + (cells >> 8)
    hot_z = one_hot(cells & 255, CZ)
    for block in range(2 * REACH + 1):
        masks[block * BLK : (block + 1) * BLK, :] = one_hot(line, BLK, block * BLK)
    bases = source_places()
    for t in range(STEPS):
        reach = 24 - 4 * t
        rows = (2 * reach + CX) * CY
        first = MID - reach * CY
        at = bases[t] + first
        hi, lo = split2(wavelet[t])
        mask = masks[first : first + rows, :]
        sources[at : at + rows, :] = dot_nt(mask * hi, hot_z) + dot_nt(mask * lo, hot_z)
    slots = got[...].T
    spans, bases = station_places()
    for block in range(2 * REACH + 1):
        words = jnp.concatenate(
            [slots[block * 8 : block * 8 + 8, :], slots[64 + block * 8 : 72 + block * 8, :]], axis=1
        )
        cells = words[6:7, :].astype(I32)
        mask = one_hot(cells >> 8, BLK)
        hot_z = one_hot(cells & 255, CZ)
        places, his, los = [], [], []
        for t in range(1, STEPS):
            lower = max(spans[t][0], block * BLK)
            upper = min(spans[t][1], block * BLK + BLK)
            if lower < upper:
                hi, lo = split2(words[t - 1 : t, :])
                wanted = mask[lower - block * BLK : upper - block * BLK]
                places.append((bases[t] + lower, upper - lower))
                his.append(wanted * hi)
                los.append(wanted * lo)
        value = dot_nt(jnp.concatenate(his, axis=0), hot_z) + dot_nt(jnp.concatenate(los, axis=0), hot_z)
        at = 0
        for place, rows in places:
            stations[place : place + rows, :] = value[at : at + rows]
            at += rows


def field_kernel(*refs):
    pieces, refs = refs[:7], refs[7:]
    sources, stations, band = refs[:3]
    keep, send, norms = refs[3:6]
    wide, rim_a, rim_b, field_a, field_b, high, low, drive, total, part, z_part = refs[6:]
    me = lax.axis_index("space")
    member = lax.axis_index("batch")
    halves = [slice(0, 128), slice(128, 256)]

    def along(slot, x, rows):
        at = rows_at(x, rows)
        z_part[0 : rows * CY, :] = dot(high[slot, at, :], band[...]) + dot(low[slot, at, :], band[...])

    bases = source_places()
    widen_courant(pieces, wide, me)
    clear_rims(rim_a)
    clear_rims(rim_b)
    rims = (rim_a, rim_b)

    def begin(x, rows):
        for half, lanes in enumerate(halves):
            value = sources[rows_at(x, rows), lanes].reshape(rows, CY, 128)
            rim_a[pl.ds(x, rows), half, 8:24, :] = value
            store_split(high, low, 0, x, half, value, rows)

    over_chunks(24, begin)
    for t in range(1, STEPS):
        now, other, slot = rims[(t - 1) % 2], rims[t % 2], (t - 1) % 2

        def chunk(x0, count, now=now, other=other, slot=slot, t=t):
            along(slot, x0, count)
            for i, rows in pieces_of(count):
                for half in range(2):
                    part[half, i : i + rows] = laplace_xy(now, x0 + i, half, rows)
            for i, rows in pieces_of(count):
                x = x0 + i
                at = rows_at(x, rows)
                for half, lanes in enumerate(halves):
                    lap = part[half, i : i + rows]
                    lap = lap + z_part[i * CY : (i + rows) * CY, lanes].reshape(rows, CY, 128)
                    step = wide[at, lanes].reshape(rows, CY, 128) * lap
                    step = step + sources[rows_at(x, rows, bases[t]), lanes].reshape(rows, CY, 128)
                    drive[t - 1, at, lanes] = step.reshape(rows * CY, 128)
                    if t < STEPS - 1:
                        new = 2.0 * now[pl.ds(x, rows), half, 8:24, :] + step
                        if t > 1:
                            new = new - other[pl.ds(x, rows), half, 8:24, :]
                        other[pl.ds(x, rows), half, 8:24, :] = new
                        store_split(high, low, 1 - slot, x, half, new, rows)

        over_chunks(24 - 4 * t, chunk)

    _, bases = station_places()
    fields = (field_a, field_b)

    def begin_back(x0, count):
        for i, rows in pieces_of(count):
            x = x0 + i
            at = rows_at(x, rows)
            for half, lanes in enumerate(halves):
                value = stations[rows_at(x, rows, bases[6]), lanes].reshape(rows, CY, 128)
                field_a[pl.ds(x, rows), half] = value
                value = value * wide[at, lanes].reshape(rows, CY, 128)
                rim_a[pl.ds(x, rows), half, 8:24, :] = value
                store_split(high, low, 0, x, half, value, rows)

    over_chunks(20, begin_back)

    def gather(field, t, first):
        for half, lanes in enumerate(halves):
            term = field[REACH * CX : REACH * CX + CX, half].reshape(BLK, 128)
            term = term * drive[t - 1, MID : MID + BLK, lanes]
            total[:, lanes] = term if first else total[:, lanes] + term

    gather(field_a, 6, True)
    for t in range(STEPS - 2, 0, -1):
        n = STEPS - 2 - t
        now, other, slot = fields[n % 2], fields[(n + 1) % 2], n % 2
        source, target = rims[slot], rims[1 - slot]

        def chunk(x0, count, now=now, other=other, slot=slot, source=source, target=target, t=t, n=n):
            along(slot, x0, count)
            for i, rows in pieces_of(count):
                for half in range(2):
                    part[half, i : i + rows] = laplace_xy(source, x0 + i, half, rows)
            for i, rows in pieces_of(count):
                x = x0 + i
                at = rows_at(x, rows)
                for half, lanes in enumerate(halves):
                    new = part[half, i : i + rows]
                    new = new + z_part[i * CY : (i + rows) * CY, lanes].reshape(rows, CY, 128)
                    new = new + stations[rows_at(x, rows, bases[t]), lanes].reshape(rows, CY, 128)
                    new = new + 2.0 * now[pl.ds(x, rows), half]
                    if n > 0:
                        new = new - other[pl.ds(x, rows), half]
                    other[pl.ds(x, rows), half] = new
                    if t > 1:
                        new = new * wide[at, lanes].reshape(rows, CY, 128)
                        target[pl.ds(x, rows), half, 8:24, :] = new
                        store_split(high, low, 1 - slot, x, half, new, rows)

        over_chunks(4 * (t - 1), chunk)
        gather(other, t, False)
    gradient = total[...].reshape(CX, CY, CZ)
    squares = jnp.sum(jnp.sum(gradient * gradient, axis=0), axis=0, keepdims=True)
    norm = jnp.sum(squares, axis=1, keepdims=True)
    front, back = gradient[:, 0:8, :], gradient[:, 8:16, :]
    keep[...] = jnp.where(member == 0, front, back)
    send[...] = jnp.where(member == 0, back, front)
    norms[...] = jnp.broadcast_to(norm, (8, 128))


def finish_kernel(keep, other, norms, update, share):
    sums = jnp.sum(norms[...], axis=0, keepdims=True)
    cells = float(PEERS * BLK * CZ)
    mean_first = sums[0:1, 0:1] / cells
    mean_second = sums[0:1, 64:65] / cells
    scale = jnp.sqrt((mean_first + mean_second) / 2.0 + epsilon)
    update[...] = (keep[...] + other[...]) / scale.reshape(1, 1, 1)
    ratio = (mean_first + epsilon) / (mean_first + mean_second + 2.0 * epsilon)
    share[...] = jnp.broadcast_to(ratio, (1, 128))


VM = pl.BlockSpec(memory_space=pltpu.VMEM)


def call(kernel, outs, scratch, *args, flops=0, limit=4 << 20):
    size = sum(int(np.prod(a.shape)) * 4 for a in args)
    return pl.pallas_call(
        kernel,
        out_shape=outs,
        in_specs=[VM] * len(args),
        out_specs=jax.tree.map(lambda _: VM, outs),
        scratch_shapes=scratch,
        cost_estimate=pl.CostEstimate(flops=flops, bytes_accessed=size, transcendentals=0),
        compiler_params=pltpu.CompilerParams(vmem_limit_bytes=limit),
    )(*args)


def shape(*dims, dtype=F32):
    return jax.ShapeDtypeStruct(dims, dtype)


def body(courant, wavelet, source_owner, source_cell, traces, station_owner, station_cell):
    def shift(value, k):
        return lax.ppermute(value, "space", [(i, (i + k) % PEERS) for i in range(PEERS)])

    half_slab = shape(CX // 2, CY, CZ)
    sent, front, back = call(
        prep_kernel,
        (shape(ROWS, 128), half_slab, half_slab),
        [pltpu.VMEM((8, ROWS), F32), pltpu.VMEM((ROWS + 32, 128), F32)],
        jnp.transpose(traces, (2, 0, 1)),
        station_owner.reshape(1, ROWS),
        station_cell,
        courant,
        flops=10**8,
        limit=None,
    )
    pieces = [courant]
    for k in range(1, REACH + 1):
        below, above = (back, front) if k == REACH else (courant, courant)
        pieces += [shift(below, k), shift(above, -k)]
    got = lax.all_to_all(sent.reshape(PEERS, 4, 128), "space", split_axis=0, concat_axis=0, tiled=True)
    sources, stations = call(
        inject_kernel,
        (shape(28 * BLK, CZ), shape(21 * BLK, CZ)),
        [pltpu.VMEM((EXT, CZ), BF16)],
        jnp.transpose(wavelet, (2, 0, 1)),
        source_owner,
        source_cell,
        got.reshape(ROWS, 128),
        flops=4 * 10**9,
        limit=12 << 20,
    )
    keep, send, mine = call(
        field_kernel,
        (shape(CX, 8, CZ), shape(CX, 8, CZ), shape(8, 128)),
        [pltpu.VMEM((EXT, CZ), F32)]
        + [pltpu.VMEM((WIDE, 2, 32, 128), F32)] * 2
        + [pltpu.VMEM((WIDE, 2, CY, 128), F32)] * 2
        + [pltpu.VMEM((2, EXT, CZ), BF16)] * 2
        + [pltpu.VMEM((STEPS - 1, EXT, CZ), F32), pltpu.VMEM((BLK, CZ), F32)]
        + [pltpu.VMEM((2, 24, CY, 128), F32), pltpu.VMEM((24 * CY, CZ), F32)],
        *pieces,
        sources,
        stations,
        jnp.asarray(band_z()),
        flops=4 * 10**9,
        limit=30 << 20,
    )
    swap = [(0, 1), (1, 0)]
    theirs = lax.ppermute(mine, "batch", swap)
    other = lax.ppermute(send, "batch", swap)
    lanes = lax.broadcasted_iota(I32, (8, 128), 1) < 64
    row = jnp.where(lanes == (lax.axis_index("batch") == 0), mine, theirs)
    partial = jnp.broadcast_to(row[0:1][None], (PEERS, 1, 128))
    norms = lax.all_to_all(partial, "space", split_axis=0, concat_axis=0, tiled=True)
    update, share = call(
        finish_kernel, (shape(CX, 8, CZ), shape(1, 128)), [], keep, other, norms.reshape(PEERS, 128)
    )
    return update, share[0, 0:1]


def solution(mesh):
    placed = (
        P("space", None, None),
        P("batch", None, None),
        P("batch", None),
        P("batch", None),
        P("batch", "space", None),
        P("batch", "space", None),
        P("batch", "space"),
    )
    return jax.shard_map(
        body,
        mesh=mesh,
        in_specs=placed,
        out_specs=(P("space", "batch", None), P()),
        check_vma=False,
    )
```

```python
import jax
import jax.numpy as jnp
import numpy as np
from jax import lax
from jax.experimental import pallas as pl
from jax.experimental.pallas import tpu as pltpu
from jax.sharding import PartitionSpec as P


F32, BF16, I32 = jnp.float32, jnp.bfloat16, jnp.int32
epsilon = 1e-06

CX, CY, CZ = 8, 16, 256
BLK = CX * CY
REACH = 3
EXT = (2 * REACH + 1) * BLK
MID = REACH * BLK
WIDE = (2 * REACH + 1) * CX
STEPS = 7
ROWS = 256
SLOTS = 8
PEERS = 64


def split2(x):
    hi = x.astype(BF16)
    return hi, (x - hi.astype(F32)).astype(BF16)


SCALE = 1.6 / 63.0
TAPS = (63.0, -7.875, 1.0, -9.0 / 128.0)
CENTRE_XY, CENTRE_Z = -336.0, -21.0 / 64.0


def band_z():
    band = np.zeros((CZ, CZ), np.float64)
    for z in range(CZ):
        band[z, z] = CENTRE_Z
        for k in range(1, 5):
            for other in (z + k, z - k):
                if 0 <= other < CZ:
                    band[other, z] = TAPS[k - 1]
    return band.astype(jnp.bfloat16)


def dot(a, b):
    return lax.dot_general(a, b, (((1,), (0,)), ((), ())), preferred_element_type=F32)


def dot_nt(a, b):
    return lax.dot_general(a, b, (((1,), (1,)), ((), ())), preferred_element_type=F32)


def one_hot(index_row, height, base=0):
    iota = lax.broadcasted_iota(I32, (height, index_row.shape[1]), 0) + base
    return jnp.where(iota == index_row, 1.0, 0.0).astype(BF16)


def prep_kernel(traces, owner, cell, out, words, padded):
    own = owner[...]
    own_f = own.astype(F32)
    column = jnp.broadcast_to(own_f, (128, ROWS)).T
    column = jnp.concatenate([column, column], axis=1)
    first = lax.broadcasted_iota(I32, (ROWS, ROWS), 0)
    second = lax.broadcasted_iota(I32, (ROWS, ROWS), 1)
    same = (column == jnp.broadcast_to(own_f, (ROWS, ROWS))) & (first < second)
    rank = jnp.sum(jnp.where(same, 1.0, 0.0), axis=0, keepdims=True).astype(I32)
    half = SLOTS // 2
    low = rank < half
    place = own * half + jnp.where(low, rank, rank - half)
    hot_low = one_hot(jnp.where(low, place, -1), PEERS * half)
    hot_high = one_hot(jnp.where(low, -1, place), PEERS * half)
    hot = jnp.concatenate([hot_low, hot_high], axis=1)
    for t in range(1, STEPS):
        words[t - 1 : t, :] = traces[t]
    words[6:7, :] = cell[...].astype(F32)
    words[7:8, :] = jnp.zeros((1, ROWS), F32)
    rest = words[...]
    total = None
    for _ in range(3):
        piece = rest.astype(BF16)
        rest = rest - piece.astype(F32)
        wide = jnp.concatenate([piece.astype(F32)] * 8, axis=0)
        empty = jnp.zeros_like(wide)
        both = jnp.concatenate(
            [jnp.concatenate([wide, empty], axis=1), jnp.concatenate([empty, wide], axis=1)], axis=0
        ).astype(BF16)
        part = dot_nt(hot, both)
        total = part if total is None else total + part
    edge = 16
    padded[0:edge, :] = jnp.zeros((edge, 128), F32)
    padded[edge + ROWS : edge + ROWS + edge, :] = jnp.zeros((edge, 128), F32)
    padded[edge : edge + ROWS, :] = total
    group = lax.broadcasted_iota(I32, (ROWS, 128), 1) % 64 // 8
    result = jnp.zeros((ROWS, 128), F32)
    for j in range(2 * REACH + 1):
        start = edge + half * (j - REACH)
        result = jnp.where(group == j, padded[start : start + ROWS, :], result)
    out[...] = result


def widen_courant(pieces, wide, me):
    wide[0:64, :] = jnp.zeros((64, CZ), F32)
    wide[EXT - 64 : EXT, :] = jnp.zeros((64, CZ), F32)
    wide[MID : MID + BLK, :] = pieces[0][...].reshape(BLK, CZ) * SCALE
    _, below, above, lower, upper = pieces

    def inside(k):
        return jnp.where((me + k >= 0) & (me + k < PEERS), SCALE, 0.0)

    half = BLK // 2
    wide[half:BLK, :] = lower[0 : CX // 2].reshape(half, CZ) * inside(-3)
    wide[BLK : 2 * BLK, :] = lower[CX // 2 :].reshape(BLK, CZ) * inside(-2)
    wide[2 * BLK : MID, :] = below[...].reshape(BLK, CZ) * inside(-1)
    wide[MID + BLK : MID + 2 * BLK, :] = above[...].reshape(BLK, CZ) * inside(1)
    wide[MID + 2 * BLK : MID + 3 * BLK, :] = upper[0:CX].reshape(BLK, CZ) * inside(2)
    wide[MID + 3 * BLK : MID + 3 * BLK + half, :] = upper[CX:].reshape(half, CZ) * inside(3)


def clear_rims(field):
    rim = jnp.zeros((WIDE, 2, 8, 128), F32)
    field[:, :, 0:8, :] = rim
    field[:, :, 24:32, :] = rim


def laplace_xy(field, x, half, rows):
    centre = field[pl.ds(x, rows), half, 8:24, :]
    out = CENTRE_XY * centre
    for k in range(1, 5):
        pairs = field[pl.ds(x + k, rows), half, 8:24, :] + field[pl.ds(x - k, rows), half, 8:24, :]
        pairs = pairs + field[pl.ds(x, rows), half, 8 + k : 24 + k, :]
        pairs = pairs + field[pl.ds(x, rows), half, 8 - k : 24 - k, :]
        out = out + TAPS[k - 1] * pairs
    return out


def rows_at(x, rows, base=0):
    return pl.ds(pl.multiple_of(base + x * CY, 64), rows * CY)


def store_split(high, low, slot, x, half, value, rows):
    hi, lo = split2(value.reshape(rows * CY, 128))
    at = rows_at(x, rows)
    lanes = slice(half * 128, half * 128 + 128)
    high[slot, at, lanes], low[slot, at, lanes] = hi, lo


TRIP = {56: 28, 48: 24, 40: 20, 32: 16, 24: 24, 16: 16, 8: 8}


def over_chunks(beyond, chunk):
    total = 2 * beyond + CX
    rows = TRIP[total]

    def step(i, carry):
        chunk(REACH * CX - beyond + rows * i, rows)
        return carry

    if rows == total:
        step(0, 0)
    else:
        lax.fori_loop(0, total // rows, step, 0)


def pieces_of(rows):
    return [(i, min(CX, rows - i)) for i in range(0, rows, CX)]


def join_kernel(courant, below, above, lower, upper):
    lower[0 : CX // 2] = below[CX // 2 :]
    lower[CX // 2 :] = courant[...]
    upper[0:CX] = courant[...]
    upper[CX:] = above[0 : CX // 2]


def source_places():
    bases, at = [], 0
    for t in range(STEPS):
        reach = 24 - 4 * t
        bases.append(at - (MID - reach * CY))
        at += (2 * reach + CX) * CY
    return bases


def station_places():
    spans, bases, at = {}, {}, 0
    for t in range(1, STEPS):
        reach = 4 * (t - 1)
        spans[t] = (MID - reach * CY, MID + BLK + reach * CY)
        bases[t] = at - spans[t][0]
        at += spans[t][1] - spans[t][0]
    return spans, bases


def inject_kernel(wavelet, owner, cell, got, sources, stations, masks):
    me = lax.axis_index("space")
    cells = cell[...]
    line = (owner[...] - me + REACH) * BLK + (cells >> 8)
    hot_z = one_hot(cells & 255, CZ)
    for block in range(2 * REACH + 1):
        masks[block * BLK : (block + 1) * BLK, :] = one_hot(line, BLK, block * BLK)
    bases = source_places()
    for t in range(STEPS):
        reach = 24 - 4 * t
        rows = (2 * reach + CX) * CY
        first = MID - reach * CY
        at = bases[t] + first
        hi, lo = split2(wavelet[t])
        mask = masks[first : first + rows, :]
        sources[at : at + rows, :] = dot_nt(mask * hi, hot_z) + dot_nt(mask * lo, hot_z)
    slots = got[...].T
    spans, bases = station_places()
    for block in range(2 * REACH + 1):
        words = jnp.concatenate(
            [slots[block * 8 : block * 8 + 8, :], slots[64 + block * 8 : 72 + block * 8, :]], axis=1
        )
        cells = words[6:7, :].astype(I32)
        mask = one_hot(cells >> 8, BLK)
        hot_z = one_hot(cells & 255, CZ)
        places, his, los = [], [], []
        for t in range(1, STEPS):
            lower = max(spans[t][0], block * BLK)
            upper = min(spans[t][1], block * BLK + BLK)
            if lower < upper:
                hi, lo = split2(words[t - 1 : t, :])
                wanted = mask[lower - block * BLK : upper - block * BLK]
                places.append((bases[t] + lower, upper - lower))
                his.append(wanted * hi)
                los.append(wanted * lo)
        value = dot_nt(jnp.concatenate(his, axis=0), hot_z) + dot_nt(jnp.concatenate(los, axis=0), hot_z)
        at = 0
        for place, rows in places:
            stations[place : place + rows, :] = value[at : at + rows]
            at += rows


def field_kernel(*refs):
    pieces, refs = refs[:5], refs[5:]
    sources, stations, band = refs[:3]
    keep, send, norms = refs[3:6]
    wide, rim_a, rim_b, field_a, field_b, high, low, drive, total, part, z_part = refs[6:]
    me = lax.axis_index("space")
    member = lax.axis_index("batch")
    halves = [slice(0, 128), slice(128, 256)]

    def along(slot, x, rows):
        at = rows_at(x, rows)
        z_part[0 : rows * CY, :] = dot(high[slot, at, :], band[...]) + dot(low[slot, at, :], band[...])

    bases = source_places()
    widen_courant(pieces, wide, me)
    clear_rims(rim_a)
    clear_rims(rim_b)
    rims = (rim_a, rim_b)

    def begin(x, rows):
        for half, lanes in enumerate(halves):
            value = sources[rows_at(x, rows), lanes].reshape(rows, CY, 128)
            rim_a[pl.ds(x, rows), half, 8:24, :] = value
            store_split(high, low, 0, x, half, value, rows)

    over_chunks(24, begin)
    for t in range(1, STEPS):
        now, other, slot = rims[(t - 1) % 2], rims[t % 2], (t - 1) % 2

        def chunk(x0, count, now=now, other=other, slot=slot, t=t):
            along(slot, x0, count)
            for i, rows in pieces_of(count):
                for half in range(2):
                    part[half, i : i + rows] = laplace_xy(now, x0 + i, half, rows)
            for i, rows in pieces_of(count):
                x = x0 + i
                at = rows_at(x, rows)
                for half, lanes in enumerate(halves):
                    lap = part[half, i : i + rows]
                    lap = lap + z_part[i * CY : (i + rows) * CY, lanes].reshape(rows, CY, 128)
                    step = wide[at, lanes].reshape(rows, CY, 128) * lap
                    step = step + sources[rows_at(x, rows, bases[t]), lanes].reshape(rows, CY, 128)
                    drive[t - 1, at, lanes] = step.reshape(rows * CY, 128)
                    if t < STEPS - 1:
                        new = 2.0 * now[pl.ds(x, rows), half, 8:24, :] + step
                        if t > 1:
                            new = new - other[pl.ds(x, rows), half, 8:24, :]
                        other[pl.ds(x, rows), half, 8:24, :] = new
                        store_split(high, low, 1 - slot, x, half, new, rows)

        over_chunks(24 - 4 * t, chunk)

    _, bases = station_places()
    fields = (field_a, field_b)

    def begin_back(x0, count):
        for i, rows in pieces_of(count):
            x = x0 + i
            at = rows_at(x, rows)
            for half, lanes in enumerate(halves):
                value = stations[rows_at(x, rows, bases[6]), lanes].reshape(rows, CY, 128)
                field_a[pl.ds(x, rows), half] = value
                value = value * wide[at, lanes].reshape(rows, CY, 128)
                rim_a[pl.ds(x, rows), half, 8:24, :] = value
                store_split(high, low, 0, x, half, value, rows)

    over_chunks(20, begin_back)

    def gather(field, t, first):
        for half, lanes in enumerate(halves):
            term = field[REACH * CX : REACH * CX + CX, half].reshape(BLK, 128)
            term = term * drive[t - 1, MID : MID + BLK, lanes]
            total[:, lanes] = term if first else total[:, lanes] + term

    gather(field_a, 6, True)
    for t in range(STEPS - 2, 0, -1):
        n = STEPS - 2 - t
        now, other, slot = fields[n % 2], fields[(n + 1) % 2], n % 2
        source, target = rims[slot], rims[1 - slot]

        def chunk(x0, count, now=now, other=other, slot=slot, source=source, target=target, t=t, n=n):
            along(slot, x0, count)
            for i, rows in pieces_of(count):
                for half in range(2):
                    part[half, i : i + rows] = laplace_xy(source, x0 + i, half, rows)
            for i, rows in pieces_of(count):
                x = x0 + i
                at = rows_at(x, rows)
                for half, lanes in enumerate(halves):
                    new = part[half, i : i + rows]
                    new = new + z_part[i * CY : (i + rows) * CY, lanes].reshape(rows, CY, 128)
                    new = new + stations[rows_at(x, rows, bases[t]), lanes].reshape(rows, CY, 128)
                    new = new + 2.0 * now[pl.ds(x, rows), half]
                    if n > 0:
                        new = new - other[pl.ds(x, rows), half]
                    other[pl.ds(x, rows), half] = new
                    if t > 1:
                        new = new * wide[at, lanes].reshape(rows, CY, 128)
                        target[pl.ds(x, rows), half, 8:24, :] = new
                        store_split(high, low, 1 - slot, x, half, new, rows)

        over_chunks(4 * (t - 1), chunk)
        gather(other, t, False)
    gradient = total[...].reshape(CX, CY, CZ)
    squares = jnp.sum(jnp.sum(gradient * gradient, axis=0), axis=0, keepdims=True)
    norm = jnp.sum(squares, axis=1, keepdims=True)
    front, back = gradient[:, 0:8, :], gradient[:, 8:16, :]
    keep[...] = jnp.where(member == 0, front, back)
    send[...] = jnp.where(member == 0, back, front)
    norms[...] = jnp.broadcast_to(norm, (8, 128))


def finish_kernel(keep, other, norms, update, share):
    sums = jnp.sum(norms[...], axis=0, keepdims=True)
    cells = float(PEERS * BLK * CZ)
    mean_first = sums[0:1, 0:1] / cells
    mean_second = sums[0:1, 64:65] / cells
    scale = jnp.sqrt((mean_first + mean_second) / 2.0 + epsilon)
    update[...] = (keep[...] + other[...]) / scale.reshape(1, 1, 1)
    ratio = (mean_first + epsilon) / (mean_first + mean_second + 2.0 * epsilon)
    share[...] = jnp.broadcast_to(ratio, (1, 128))


VM = pl.BlockSpec(memory_space=pltpu.VMEM)


def call(kernel, outs, scratch, *args, flops=0, limit=4 << 20):
    size = sum(int(np.prod(a.shape)) * 4 for a in args)
    return pl.pallas_call(
        kernel,
        out_shape=outs,
        in_specs=[VM] * len(args),
        out_specs=jax.tree.map(lambda _: VM, outs),
        scratch_shapes=scratch,
        cost_estimate=pl.CostEstimate(flops=flops, bytes_accessed=size, transcendentals=0),
        compiler_params=pltpu.CompilerParams(vmem_limit_bytes=limit),
    )(*args)


def shape(*dims, dtype=F32):
    return jax.ShapeDtypeStruct(dims, dtype)


def body(courant, wavelet, source_owner, source_cell, traces, station_owner, station_cell):
    def shift(value, k):
        return lax.ppermute(value, "space", [(i, (i + k) % PEERS) for i in range(PEERS)])

    sent = call(
        prep_kernel,
        shape(ROWS, 128),
        [pltpu.VMEM((8, ROWS), F32), pltpu.VMEM((ROWS + 32, 128), F32)],
        jnp.transpose(traces, (2, 0, 1)),
        station_owner.reshape(1, ROWS),
        station_cell,
        flops=10**8,
        limit=None,
    )
    below, above = shift(courant, 1), shift(courant, -1)
    taller = shape(CX + CX // 2, CY, CZ)
    lower, upper = call(join_kernel, (taller, taller), [], courant, below, above)
    pieces = [courant, below, above, shift(lower, 2), shift(upper, -2)]
    got = lax.all_to_all(sent.reshape(PEERS, 4, 128), "space", split_axis=0, concat_axis=0, tiled=True)
    sources, stations = call(
        inject_kernel,
        (shape(28 * BLK, CZ), shape(21 * BLK, CZ)),
        [pltpu.VMEM((EXT, CZ), BF16)],
        jnp.transpose(wavelet, (2, 0, 1)),
        source_owner,
        source_cell,
        got.reshape(ROWS, 128),
        flops=4 * 10**9,
        limit=12 << 20,
    )
    keep, send, mine = call(
        field_kernel,
        (shape(CX, 8, CZ), shape(CX, 8, CZ), shape(8, 128)),
        [pltpu.VMEM((EXT, CZ), F32)]
        + [pltpu.VMEM((WIDE, 2, 32, 128), F32)] * 2
        + [pltpu.VMEM((WIDE, 2, CY, 128), F32)] * 2
        + [pltpu.VMEM((2, EXT, CZ), BF16)] * 2
        + [pltpu.VMEM((STEPS - 1, EXT, CZ), F32), pltpu.VMEM((BLK, CZ), F32)]
        + [pltpu.VMEM((2, 24, CY, 128), F32), pltpu.VMEM((24 * CY, CZ), F32)],
        *pieces,
        sources,
        stations,
        jnp.asarray(band_z()),
        flops=4 * 10**9,
        limit=30 << 20,
    )
    swap = [(0, 1), (1, 0)]
    theirs = lax.ppermute(mine, "batch", swap)
    other = lax.ppermute(send, "batch", swap)
    lanes = lax.broadcasted_iota(I32, (8, 128), 1) < 64
    row = jnp.where(lanes == (lax.axis_index("batch") == 0), mine, theirs)
    partial = jnp.broadcast_to(row[0:1][None], (PEERS, 1, 128))
    norms = lax.all_to_all(partial, "space", split_axis=0, concat_axis=0, tiled=True)
    update, share = call(
        finish_kernel, (shape(CX, 8, CZ), shape(1, 128)), [], keep, other, norms.reshape(PEERS, 128)
    )
    return update, share[0, 0:1]


def solution(mesh):
    placed = (
        P("space", None, None),
        P("batch", None, None),
        P("batch", None),
        P("batch", None),
        P("batch", "space", None),
        P("batch", "space", None),
        P("batch", "space"),
    )
    return jax.shard_map(
        body,
        mesh=mesh,
        in_specs=placed,
        out_specs=(P("space", "batch", None), P()),
        check_vma=False,
    )
```
